512 devices in a mesh: leaf: 128 (over x_hi, z, y), sub: 4 (over x_lo, core).
Axes of the slice: x: 4 (x_hi: 2, x_lo: 2; x = x_hi * 2 + x_lo), y: 4, z: 16, core: 2. Of those that a mesh axis runs over, the one named last changes fastest.
Arguments:
- points: float32 [16384, 3, 128], P(('leaf', 'sub')), may hold values from 0 to 1
- charges: float32 [16384, 8, 128], P(('leaf', 'sub')), may hold values from -6 to 6
- leaf_skel: float32 [16384, 3, 64], P(('leaf', 'sub')), may hold values from 0 to 1
- mid_skel: float32 [2048, 3, 64], P(('leaf', 'sub')), may hold values from 0 to 1
- root_skel: float32 [128, 3, 64], replicated, may hold values from 0 to 1
- leaf_transfer: float32 [16384, 64, 64], P(('leaf', 'sub')), may hold values from -0.25 to 0.25
- mid_transfer: float32 [2048, 64, 64], P(('leaf', 'sub')), may hold values from -0.75 to 0.75
- near_list: int32 [16384, 27], P(('leaf', 'sub')), may hold values from -1 to 16383, as said below
- far_list: int32 [16384, 20], P(('leaf', 'sub')), may hold values from -1 to 16383, as said below
- mid_list: int32 [2048, 6], P(('leaf', 'sub')), may hold values from -1 to 2047, as said below
- root_list: int32 [128, 6], P('leaf'), may hold values from -1 to 127, as said below
Outputs:
- potentials: float32 [16384, 8, 128], P(('leaf', 'sub'))
The draws below stay inside these ranges and needn't reach their ends.
Inputs may be any that keep to these rules, and one draw needn't show every extreme that they name: `near_list`: slot 0 of a leaf's row is the leaf itself. Every other entry is -1 or a leaf other than itself that lies on the same device or on one of the two devices beside it in the order of leaf indices; no leaf appears twice in the near and coupling rows of one leaf together. `far_list`: every entry is -1 or a leaf other than the row's own that lies on the same device or on one of the two devices beside it in the order of leaf indices, never one of the row's near_list entries. `mid_list`: every entry is -1 or a middle cluster other than the row's own under the same subtree root, at most once in a row. `root_list`: every entry is -1 or a root other than the row's own, at most once in a row.
All inputs are finite; a program needn't handle non-finite values.
Results may differ from the reference program's by a relative error of at most 0.0003.
Values sent between devices are 32-bit elements; how exact they have to be, the bound alone decides.
A program may use at most 64 MiB of HBM per device.

```python
import math
import jax
import jax.numpy as jnp
from jax import lax

LEAF = 128
SKELETON_RANK = 64
RIGHT_SIDES = 8
LD = 32
NEARF = 27
FARF = 20
FARM = 6
FART = 6
GM = 16
LEAF_TOTAL = 16384
MIDDLE_TOTAL = 2048
NT = 128


def choose_from(key, candidates, self_column, count):
    columns = candidates.shape[1]
    scores = jax.random.randint(key, candidates.shape, 0, 2 ** 20) * columns + jnp.arange(columns)[None, :]
    scores = jnp.where(jnp.arange(columns)[None, :] == self_column[:, None], -1, scores)
    order = jnp.argsort(-scores, axis=1)[:, :count]
    return jnp.take_along_axis(candidates, order, axis=1)


def drop_some(key, chosen, limit):
    valid = (chosen >= 0) & (chosen < limit)
    keeping = jax.random.randint(key, chosen.shape, 0, 4) > 0
    keeping = keeping.at[0, chosen.shape[1] - 1].set(False)
    return jnp.where(valid & keeping, chosen, -1).astype(jnp.int32)


def leaf_lists(key):
    folded = jax.random.fold_in(key, 11)
    row_ids = jnp.arange(LEAF_TOTAL)
    window_start = (row_ids // LD - 1) * LD
    candidates = window_start[:, None] + jnp.arange(3 * LD)[None, :]
    chosen = choose_from(jax.random.fold_in(folded, 1), candidates, row_ids - window_start, NEARF - 1 + FARF)
    chosen = drop_some(jax.random.fold_in(folded, 2), chosen, LEAF_TOTAL)
    near_rows = jnp.concatenate([row_ids[:, None].astype(jnp.int32), chosen[:, :NEARF - 1]], axis=1)
    return (near_rows, chosen[:, NEARF - 1:])


def draw_near_list(key, part):
    return leaf_lists(key)[0]


def draw_far_list(key, part):
    return leaf_lists(key)[1]


def draw_mid_list(key, part):
    folded = jax.random.fold_in(key, 23)
    row_ids = jnp.arange(MIDDLE_TOTAL)
    group_start = row_ids // GM * GM
    candidates = group_start[:, None] + jnp.arange(GM)[None, :]
    chosen = choose_from(jax.random.fold_in(folded, 1), candidates, row_ids - group_start, FARM)
    return drop_some(jax.random.fold_in(folded, 2), chosen, MIDDLE_TOTAL)


def draw_root_list(key, part):
    folded = jax.random.fold_in(key, 37)
    row_ids = jnp.arange(NT)
    candidates = jnp.broadcast_to(jnp.arange(NT)[None, :], (NT, NT))
    chosen = choose_from(jax.random.fold_in(folded, 1), candidates, row_ids, FART)
    return drop_some(jax.random.fold_in(folded, 2), chosen, NT)


def block_scale(own_key, dims, split, smallest, high):
    def one(dim, shards_of):
        heights = jax.random.uniform(jax.random.fold_in(jax.random.fold_in(own_key, 6), dim), (shards_of,), jnp.float32, smallest / len(split), high / len(split))
        return jnp.repeat(jnp.exp(heights), dims[dim] // shards_of).reshape((-1,) + (1,) * (len(dims) - dim - 1))

    factor_of = one(*split[0])
    for cut in split[1:]:
        factor_of = factor_of * one(*cut)
    return factor_of


def scatter_about(stream_key, extent, width, most, pieces=(), held_as=jnp.bfloat16):
    entries = jax.random.normal(stream_key, extent, jnp.float32) * width
    if len(pieces) > 0:
        entries = block_scale(stream_key, extent, pieces, -0.22, 0.18) * entries
    return jnp.clip(entries, min=-most, max=most).astype(held_as)


def setup_inputs(seed: int = 0) -> dict:
    streams_of = jax.random.split(jax.random.key(seed), 12)
    return {
        "points": jnp.clip(1.0 * jax.random.uniform(streams_of[0], (LEAF_TOTAL, 3, LEAF), jnp.float32) ** block_scale(streams_of[0], (LEAF_TOTAL, 3, LEAF), ((0, 512),), -0.2, 0.2), 0.0, 1.0),
        "charges": scatter_about(streams_of[1], (LEAF_TOTAL, RIGHT_SIDES, LEAF), 1.0, 6.0, ((0, 512),), jnp.float32),
        "leaf_skel": jnp.clip(1.0 * jax.random.uniform(streams_of[2], (LEAF_TOTAL, 3, SKELETON_RANK), jnp.float32) ** block_scale(streams_of[2], (LEAF_TOTAL, 3, SKELETON_RANK), ((0, 512),), -0.2, 0.2), 0.0, 1.0),
        "mid_skel": jnp.clip(1.0 * jax.random.uniform(streams_of[3], (MIDDLE_TOTAL, 3, SKELETON_RANK), jnp.float32) ** block_scale(streams_of[3], (MIDDLE_TOTAL, 3, SKELETON_RANK), ((0, 512),), -0.2, 0.2), 0.0, 1.0),
        "root_skel": jnp.clip(jax.random.uniform(streams_of[4], (NT, 3, SKELETON_RANK), jnp.float32, 0.0, 1.0), 0.0, 1.0),
        "leaf_transfer": scatter_about(streams_of[5], (LEAF_TOTAL, SKELETON_RANK, SKELETON_RANK), (8 * SKELETON_RANK) ** -0.5, 0.25, ((0, 512),), jnp.float32),
        "mid_transfer": scatter_about(streams_of[6], (MIDDLE_TOTAL, SKELETON_RANK, SKELETON_RANK), SKELETON_RANK ** -0.5, 0.75, ((0, 512),), jnp.float32),
        "near_list": draw_near_list(jax.random.fold_in(streams_of[11], 71), 0),
        "far_list": draw_far_list(jax.random.fold_in(streams_of[11], 71), 0),
        "mid_list": draw_mid_list(jax.random.fold_in(streams_of[11], 71), 0),
        "root_list": draw_root_list(jax.random.fold_in(streams_of[11], 71), 0),
    }


DELTA2 = 0.0025
EXACT_PRECISION = lax.Precision.HIGHEST

def kernel(targets, sources):
    first = targets[:, 0, :, None] - sources[:, 0, None, :]
    second = targets[:, 1, :, None] - sources[:, 1, None, :]
    third = targets[:, 2, :, None] - sources[:, 2, None, :]
    return 1.0 / jnp.sqrt(first * first + second * second + third * third + DELTA2)

def lookup(table, partner_idx):
    present = (partner_idx >= 0).astype(jnp.float32)
    position = jnp.clip(partner_idx, 0, table.shape[0] - 1).astype(jnp.int32)
    return (table[position], present)

def couple(target_skel, coeff_table, skel_table, lists, scale):

    def add_slot(slot_no, running):
        partner_idx = lax.dynamic_slice_in_dim(lists, slot_no, 1, 1)[:, 0]
        partner_coeffs, present = lookup(coeff_table, partner_idx)
        partner_skel, unused = lookup(skel_table, partner_idx)
        matrix = kernel(target_skel, partner_skel)
        term = jnp.einsum('lab,lrb->lra', matrix, partner_coeffs, precision=EXACT_PRECISION)
        return running + term * (present * scale)[:, None, None]
    start_value = jnp.zeros((target_skel.shape[0], coeff_table.shape[1], coeff_table.shape[2]), jnp.float32)
    return lax.fori_loop(0, lists.shape[1], add_slot, start_value)

def reference(points, charges, leaf_skel, mid_skel, root_skel, leaf_transfer, mid_transfer, near_list, far_list, mid_list, root_list):
    leaf_scale = 1.0 / math.sqrt(LEAF)
    rank_scale = 1.0 / SKELETON_RANK
    block_ids = jnp.arange(LEAF_TOTAL // LD, dtype=jnp.int32)

    def near_block(block_no):
        first_row = (block_no * LD).astype(jnp.int32)
        own_points = lax.dynamic_slice_in_dim(points, first_row, LD, 0)
        own_list = lax.dynamic_slice_in_dim(near_list, first_row, LD, 0)

        def add_near(slot_no, running):
            partner_idx = lax.dynamic_slice_in_dim(own_list, slot_no, 1, 1)[:, 0]
            partner_points, present = lookup(points, partner_idx)
            partner_charges, unused = lookup(charges, partner_idx)
            matrix = kernel(own_points, partner_points)
            term = jnp.einsum('lpq,lrq->lrp', matrix, partner_charges, precision=EXACT_PRECISION)
            return running + term * (present / LEAF)[:, None, None]
        return lax.fori_loop(0, NEARF, add_near, jnp.zeros((LD, RIGHT_SIDES, LEAF), jnp.float32))
    near = lax.map(near_block, block_ids).reshape(LEAF_TOTAL, RIGHT_SIDES, LEAF)
    basis = kernel(points, leaf_skel)
    expansion_weights = jnp.einsum('lpa,lrp->lra', basis, charges, precision=EXACT_PRECISION) * leaf_scale

    def far_block(block_no):
        first_row = (block_no * LD).astype(jnp.int32)
        own_skel = lax.dynamic_slice_in_dim(leaf_skel, first_row, LD, 0)
        own_list = lax.dynamic_slice_in_dim(far_list, first_row, LD, 0)
        return couple(own_skel, expansion_weights, leaf_skel, own_list, rank_scale)
    leaf_potential_field = lax.map(far_block, block_ids).reshape(LEAF_TOTAL, RIGHT_SIDES, SKELETON_RANK)
    leaf_cluster_groups = leaf_transfer.reshape(MIDDLE_TOTAL, 8, SKELETON_RANK, SKELETON_RANK)
    middle_expansion_weights = jnp.einsum('hpsi,hpds->hdi', leaf_cluster_groups, expansion_weights.reshape(MIDDLE_TOTAL, 8, RIGHT_SIDES, SKELETON_RANK), precision=EXACT_PRECISION)
    mid_field = couple(mid_skel, middle_expansion_weights, mid_skel, mid_list, rank_scale)
    mid_groups = mid_transfer.reshape(NT, GM, SKELETON_RANK, SKELETON_RANK)
    root_coeffs = jnp.einsum('tkab,tkra->trb', mid_groups, middle_expansion_weights.reshape(NT, GM, RIGHT_SIDES, SKELETON_RANK), precision=EXACT_PRECISION)
    root_field = couple(root_skel, root_coeffs, root_skel, root_list, rank_scale)
    middle_potential_total = mid_field + jnp.einsum('tkab,trb->tkra', mid_groups, root_field, precision=EXACT_PRECISION).reshape(MIDDLE_TOTAL, RIGHT_SIDES, SKELETON_RANK)
    leaf_potential_total = leaf_potential_field + jnp.einsum('oxgc,osc->oxsg', leaf_cluster_groups, middle_potential_total, precision=EXACT_PRECISION).reshape(LEAF_TOTAL, RIGHT_SIDES, SKELETON_RANK)
    return near + jnp.einsum('lpa,lra->lrp', basis, leaf_potential_total, precision=EXACT_PRECISION) * leaf_scale
```

```python
import functools
import math

import jax
import jax.numpy as jnp
from jax import lax
from jax.experimental import pallas as pl
from jax.experimental.pallas import tpu as pltpu
from jax.sharding import PartitionSpec as P

DELTA2 = 0.0025
MESH = pl.DeviceIdType.MESH
BF = jnp.bfloat16
F32 = jnp.float32
TN = (((0,), (1,)), ((), ()))
TT = (((0,), (0,)), ((), ()))
NT = (((1,), (1,)), ((), ()))
YS, ZS, XS, SUBS = 4, 16, 2, 4


def rows_of(x):
    return lax.broadcasted_iota(jnp.int32, x.shape, 0)


def low_half(shape):
    return lax.broadcasted_iota(jnp.int32, shape, len(shape) - 1) < 64


def split2(x):
    high = x.astype(BF)
    return high, (x - high.astype(F32)).astype(BF)


def stacked(x):
    high = x.astype(BF).astype(F32)
    return jnp.concatenate([high, x - high], axis=0).astype(BF)


def split3(x):
    first = x.astype(BF).astype(F32)
    rest = x - first
    second = rest.astype(BF).astype(F32)
    return first, second, (rest - second).astype(BF).astype(F32)


def centred(p):
    c = p - 0.5
    return jnp.concatenate([c, jnp.sum(c * c, axis=0, keepdims=True) + 0.5 * DELTA2], axis=0)


def doubled(s):
    return jnp.concatenate([s, s], axis=1)


def source_rows(p8):
    p1, p2, p3 = split3(p8)
    norm = (rows_of(p8) & 3) == 3
    ones = jnp.where(norm, 1.0, p1)
    return jnp.concatenate([p1, p2, p3, ones, jnp.where(norm, 1.0, p2), ones], axis=0).astype(BF)


def target_rows(p8, first_half):
    p1, p2, p3 = split3(p8)
    row = rows_of(p8)
    norm = (row & 3) == 3
    active = ((row < 4) if first_half else (row >= 4)).astype(F32)
    lead = jnp.where(norm, 1.0, -2.0 * p1) * active
    return jnp.concatenate(
        [
            lead,
            lead,
            lead,
            jnp.where(norm, p1, -2.0 * p2) * active,
            jnp.where(norm, p2, -2.0 * p2) * active,
            jnp.where(norm, p3, -2.0 * p3) * active,
        ],
        axis=0,
    )


def split_dot(two, matrix, dims):
    high, low = split2(matrix)
    out = lax.dot_general(two, high, dims, preferred_element_type=F32) + lax.dot_general(
        two, low, dims, preferred_element_type=F32
    )
    half = out.shape[0] // 2
    return out[:half] + out[half:]


NN = (((1,), (0,)), ((), ()))


def upward(
    points, charges, leaf_skel, mid_skel, leaf_transfer, mid_transfer,
    win, cwin, mids, roots, rpart, yroots, send, recv,
):
    leaf, sub = lax.axis_index("leaf"), lax.axis_index("sub")
    leaves = points.shape[0]
    nleaf = XS * ZS * YS
    flat = leaf * SUBS + sub
    total = nleaf * SUBS
    x, z, y = leaf // (ZS * YS), (leaf // YS) % ZS, leaf % YS
    right, left = (flat + 1) % total, (flat + total - 1) % total
    right_id, left_id = (right // SUBS, right % SUBS), (left // SUBS, left % SUBS)
    sub_ids = [(leaf, (sub + k) % SUBS) for k in range(1, SUBS)]
    y_ids = [(leaf - y + (y + k) % YS, sub) for k in range(1, YS)]
    z_ids = [((x * ZS + (z + k) % ZS) * YS + y, sub) for k in range(1, ZS)]
    x_id = (((1 - x) * ZS + z) * YS + y, sub)

    barrier = pltpu.get_barrier_semaphore()
    partners = [right_id, left_id] + sub_ids + y_ids + z_ids + [x_id]
    for partner in partners:
        pl.semaphore_signal(barrier, inc=1, device_id=partner, device_id_type=MESH)

    def copy(slot, src, dst, target):
        return pltpu.make_async_remote_copy(
            src_ref=src, dst_ref=dst, send_sem=send.at[slot], recv_sem=recv.at[slot],
            device_id=target, device_id_type=MESH,
        )

    leaf_scale = 1.0 / math.sqrt(points.shape[2])

    def one_leaf(i, carry):
        own = centred(points[i])
        skel = centred(doubled(leaf_skel[i]))
        x_i = charges[i]
        win[leaves + i] = jnp.concatenate([own, skel, x_i], axis=0)
        src = source_rows(jnp.concatenate([own, skel], axis=0))
        tgt = target_rows(jnp.concatenate([skel, skel], axis=0), True).astype(BF)
        d2 = lax.dot_general(src, tgt, TT, preferred_element_type=F32)
        cwin[leaves + i] = split_dot(stacked(x_i), lax.rsqrt(d2), NN) * leaf_scale
        return carry

    lax.fori_loop(0, leaves, one_leaf, 0, unroll=4)

    half = low_half((8, 128))

    def lifted(low_child, high_child, pair):
        both = jnp.where(half, low_child, high_child)
        matrix = pair.reshape(128, 64)
        return split_dot(stacked(both), doubled(matrix), NN)

    my_mids = mid_skel.shape[0]
    mid_coeffs = []
    for m in range(my_mids):
        acc = jnp.zeros((8, 128), F32)
        for k in range(0, 8, 2):
            c = m * 8 + k
            acc += lifted(cwin[leaves + c], cwin[leaves + c + 1], leaf_transfer[c : c + 2])
        mid_coeffs.append(acc)
        skel = centred(doubled(mid_skel[m]))
        mids[sub * my_mids + m] = jnp.concatenate([acc, skel, skel], axis=0)
    partial = jnp.zeros((8, 128), F32)
    for m in range(0, my_mids, 2):
        partial += lifted(mid_coeffs[m], mid_coeffs[m + 1], mid_transfer[m : m + 2])
    rpart[sub] = partial

    pl.semaphore_wait(barrier, len(partners))
    sums = [copy(k, rpart.at[sub], rpart.at[sub], sub_ids[k]) for k in range(3)]
    own_mids = mids.at[pl.ds(sub * my_mids, my_mids)]
    others = [copy(3 + k, own_mids, own_mids, sub_ids[k]) for k in range(3)]
    for n, ref in ((6, win), (8, cwin)):
        own = ref.at[pl.ds(leaves, leaves)]
        others.append(copy(n, own, ref.at[pl.ds(0, leaves)], right_id))
        others.append(copy(n + 1, own, ref.at[pl.ds(2 * leaves, leaves)], left_id))
    for c in sums + others:
        c.start()
    for c in sums:
        c.wait()
    yroots[y] = (rpart[0] + rpart[1]) + (rpart[2] + rpart[3])
    stage = [copy(10 + k, yroots.at[y], yroots.at[y], y_ids[k]) for k in range(YS - 1)]
    for c in stage:
        c.start()
    for c in stage:
        c.wait()
    roots[x, z, 0] = jnp.where(half, yroots[0], yroots[1])
    roots[x, z, 1] = jnp.where(half, yroots[2], yroots[3])
    own = roots.at[x, z]
    stage = [copy(13 + k, own, own, z_ids[k]) for k in range(ZS - 1)]
    for c in stage:
        c.start()
    for c in stage:
        c.wait()
    last = copy(28, roots.at[x], roots.at[x], x_id)
    last.start()
    for c in others:
        c.wait()
    last.wait()


def downward(
    near_list, far_list, mid_list, root_list,
    win, cwin, mids, roots, root_skel, leaf_transfer, mid_transfer,
    out, src, chg, cof, fin, msrc, mcof, rsrc, rcof,
):
    leaf, sub = lax.axis_index("leaf"), lax.axis_index("sub")
    leaves = leaf_transfer.shape[0]
    my_mids = mid_transfer.shape[0]
    window = 3 * leaves
    group = SUBS * my_mids
    start = (leaf * SUBS + sub - 1) * leaves
    rank_scale = 1.0 / leaf_transfer.shape[1]
    zero = jnp.zeros((16, 128), BF)
    half = low_half((8, 128))
    lane48 = low_half((48, 128))
    lane16 = low_half((16, 128))

    def build(j, carry):
        w = win[j]
        src[j] = source_rows(w[:8])
        chg[j] = stacked(w[8:])
        cof[j] = stacked(cwin[j])
        return carry

    lax.fori_loop(0, window, build, 0, unroll=4)
    src[window] = src[0]
    chg[window] = zero
    cof[window] = zero
    for j in range(group):
        w = mids[j]
        msrc[j] = source_rows(w[8:])
        mcof[j] = stacked(w[:8])
    msrc[group] = msrc[0]
    mcof[group] = zero

    def root_p8(r):
        p4 = centred(doubled(root_skel[r]))
        return jnp.concatenate([p4, p4], axis=0)

    slots = root_list.shape[1]
    for k in range(slots):
        r = root_list[0, k]
        present = (r >= 0).astype(F32)
        r = jnp.maximum(r, 0)
        tile = roots[r // 2]
        mine = (lax.broadcasted_iota(jnp.int32, (8, 128), 1) // 64) == (r % 2)
        coeff = jnp.where(mine, tile, pltpu.roll(tile, 64, 1))
        rsrc[k] = source_rows(root_p8(r))
        rcof[k] = stacked(coeff * present)
    for k in range(slots, 8):
        rsrc[k] = rsrc[0]
        rcof[k] = zero

    def far_targets(p8):
        rows = target_rows(p8, False)
        low = low_half(rows.shape)
        pair = jnp.concatenate([jnp.where(low, rows, 0.0), jnp.where(low, 0.0, rows)], axis=0)
        return pair.T.astype(BF)

    def quad(js, table, coeffs, tgt):
        a, b, c, d = js
        s = jnp.concatenate(
            [jnp.where(lane48, table[a], table[c]), jnp.where(lane48, table[b], table[d])], axis=0
        )
        x = jnp.concatenate(
            [jnp.where(lane16, coeffs[a], coeffs[c]), jnp.where(lane16, coeffs[b], coeffs[d])],
            axis=0,
        )
        high, low = split2(lax.rsqrt(lax.dot_general(s, tgt, TN, preferred_element_type=F32)))
        return jnp.dot(x, high, preferred_element_type=F32) + jnp.dot(
            x, low, preferred_element_type=F32
        )

    def field(acc):
        s = jnp.where(half, acc[0:8] + acc[8:16], acc[16:24] + acc[24:32])
        return (s + pltpu.roll(s, 64, 1)) * rank_scale

    acc = quad((0, 1, 2, 3), rsrc, rcof, far_targets(root_p8(leaf)))
    acc += quad((4, 5, 6, 7), rsrc, rcof, far_targets(root_p8(leaf)))
    root_two = stacked(field(acc))[:, :64]

    def lowered(two, matrix):
        return split_dot(two, jnp.concatenate([matrix, matrix], axis=0), NT)

    def place(j, first, empty):
        return jnp.where(j >= 0, j - first, empty)

    mid_two = []
    for m in range(my_mids):
        js = [place(mid_list[m, k], leaf * group, group) for k in range(mid_list.shape[1])]
        js += [group] * (8 - len(js))
        tgt = far_targets(mids[sub * my_mids + m][8:])
        f = field(quad(js[:4], msrc, mcof, tgt) + quad(js[4:], msrc, mcof, tgt))
        mid_two.append(stacked(f + lowered(root_two, mid_transfer[m]))[:, :64])

    up = 0.5 * math.sqrt(128.0)
    for m in range(my_mids):

        def far_leaves(t, carry, m=m):
            for p in range(4):
                i = m * 8 + t * 4 + p
                tgt = far_targets(win[leaves + i][:8])
                acc = jnp.zeros((32, 128), F32)
                for g in range(0, far_list.shape[1], 4):
                    js = [place(far_list[i, g + k], start, window) for k in range(4)]
                    acc += quad(js, src, cof, tgt)
                fin[i] = stacked((field(acc) + lowered(mid_two[m], leaf_transfer[i])) * up)
            return carry

        lax.fori_loop(0, 2, far_leaves, 0)

    def near_leaves(t, carry):
        ids = [t * 4 + p for p in range(4)]
        rows = [win[leaves + i][:8] for i in ids]
        tgts = [target_rows(r, True).T.astype(BF) for r in rows]
        accs = [jnp.zeros((16, 128), F32)] * 4
        count = near_list.shape[1]
        for g in range(0, count, 2):
            for p, i in enumerate(ids):
                j = place(near_list[i, g], start, window)
                if g + 1 < count:
                    k = place(near_list[i, g + 1], start, window)
                    s = jnp.concatenate([src[j], src[k]], axis=1)
                    d2 = lax.dot_general(s, tgts[p], TN, preferred_element_type=F32)
                    x = jnp.concatenate([chg[j], chg[k]], axis=1)
                else:
                    own = jnp.concatenate([rows[p][:4], rows[p][:4]], axis=0)
                    basis = target_rows(own, False).T.astype(BF)
                    d2 = jnp.concatenate(
                        [
                            lax.dot_general(src[j], tgts[p], TN, preferred_element_type=F32),
                            lax.dot_general(
                                src[leaves + i], basis, TN, preferred_element_type=F32
                            ),
                        ],
                        axis=0,
                    )
                    x = jnp.concatenate([chg[j], fin[i]], axis=1)
                high, low = split2(lax.rsqrt(d2))
                accs[p] += jnp.dot(x, high, preferred_element_type=F32) + jnp.dot(
                    x, low, preferred_element_type=F32
                )
        for p, i in enumerate(ids):
            out[i] = (accs[p][:8] + accs[p][8:]) * (1.0 / 128.0)
        return carry

    lax.fori_loop(0, leaves // 4, near_leaves, 0)


def local(
    points, charges, leaf_skel, mid_skel, root_skel, leaf_transfer, mid_transfer,
    near_list, far_list, mid_list, root_list,
):
    leaves = points.shape[0]
    mids = mid_skel.shape[0]
    vmem = pl.BlockSpec(memory_space=pltpu.VMEM)
    smem = pl.BlockSpec(memory_space=pltpu.SMEM)
    shape = jax.ShapeDtypeStruct
    win, cwin, mid_table, roots = pl.pallas_call(
        upward,
        name="upward",
        out_shape=(
            shape((3 * leaves, 16, 128), F32),
            shape((3 * leaves, 8, 128), F32),
            shape((SUBS * mids, 16, 128), F32),
            shape((XS, ZS, YS // 2, 8, 128), F32),
        ),
        in_specs=[vmem] * 6,
        out_specs=(vmem,) * 4,
        scratch_shapes=[
            pltpu.VMEM((SUBS, 8, 128), F32),
            pltpu.VMEM((YS, 8, 128), F32),
            pltpu.SemaphoreType.DMA((29,)),
            pltpu.SemaphoreType.DMA((29,)),
        ],
        compiler_params=pltpu.CompilerParams(collective_id=0, has_side_effects=True),
    )(points, charges, leaf_skel, mid_skel, leaf_transfer, mid_transfer)
    window = 3 * leaves + 1
    group = SUBS * mids + 1
    return pl.pallas_call(
        downward,
        name="downward",
        out_shape=shape((leaves, 8, 128), F32),
        in_specs=[smem] * 4 + [vmem] * 7,
        out_specs=vmem,
        scratch_shapes=[
            pltpu.VMEM((window, 48, 128), BF),
            pltpu.VMEM((window, 16, 128), BF),
            pltpu.VMEM((window, 16, 128), BF),
            pltpu.VMEM((leaves, 16, 128), BF),
            pltpu.VMEM((group, 48, 128), BF),
            pltpu.VMEM((group, 16, 128), BF),
            pltpu.VMEM((8, 48, 128), BF),
            pltpu.VMEM((8, 16, 128), BF),
        ],
    )(
        near_list, far_list, mid_list, root_list,
        win, cwin, mid_table, roots.reshape(XS * ZS * YS // 2, 8, 128),
        root_skel, leaf_transfer, mid_transfer,
    )


def solution(mesh):
    both = P(("leaf", "sub"), None, None)
    lists = P(("leaf", "sub"), None)
    in_specs = (both, both, both, both, P(), both, both, lists, lists, lists, P("leaf", None))
    return jax.shard_map(local, mesh=mesh, in_specs=in_specs, out_specs=both, check_vma=False)
```

```python
import functools
import math

import jax
import jax.numpy as jnp
from jax import lax
from jax.experimental import pallas as pl
from jax.experimental.pallas import tpu as pltpu
from jax.sharding import PartitionSpec as P

DELTA2 = 0.0025
MESH = pl.DeviceIdType.MESH
BF = jnp.bfloat16
F32 = jnp.float32
TN = (((0,), (1,)), ((), ()))
TT = (((0,), (0,)), ((), ()))
NT = (((1,), (1,)), ((), ()))
YS, ZS, XS, SUBS = 4, 16, 2, 4


def rows_of(x):
    return lax.broadcasted_iota(jnp.int32, x.shape, 0)


def low_half(shape):
    return lax.broadcasted_iota(jnp.int32, shape, len(shape) - 1) < 64


def split2(x):
    high = x.astype(BF)
    return high, (x - high.astype(F32)).astype(BF)


def stacked(x):
    high = x.astype(BF).astype(F32)
    return jnp.concatenate([high, x - high], axis=0).astype(BF)


def split3(x):
    first = x.astype(BF).astype(F32)
    rest = x - first
    second = rest.astype(BF).astype(F32)
    return first, second, (rest - second).astype(BF).astype(F32)


def centred(rows):
    c = [r - 0.5 for r in rows]
    return c + [c[0] * c[0] + c[1] * c[1] + c[2] * c[2] + 0.5 * DELTA2]


def doubled(s):
    return jnp.concatenate([s, s], axis=1)


def source_rows(p8):
    p1, p2, p3 = split3(p8)
    norm = (rows_of(p8) & 3) == 3
    ones = jnp.where(norm, 1.0, p1)
    return jnp.concatenate([p1, p2, p3, ones, jnp.where(norm, 1.0, p2), ones], axis=0).astype(BF)


def target_rows(p8, first_half):
    p1, p2, p3 = split3(p8)
    row = rows_of(p8)
    norm = (row & 3) == 3
    active = ((row < 4) if first_half else (row >= 4)).astype(F32)
    lead = jnp.where(norm, 1.0, -2.0 * p1) * active
    return jnp.concatenate(
        [
            lead,
            lead,
            lead,
            jnp.where(norm, p1, -2.0 * p2) * active,
            jnp.where(norm, p2, -2.0 * p2) * active,
            jnp.where(norm, p3, -2.0 * p3) * active,
        ],
        axis=0,
    )


def split_dot(two, matrix, dims):
    high, low = split2(matrix)
    out = lax.dot_general(two, high, dims, preferred_element_type=F32) + lax.dot_general(
        two, low, dims, preferred_element_type=F32
    )
    half = out.shape[0] // 2
    return out[:half] + out[half:]


NN = (((1,), (0,)), ((), ()))
LP = 4


def body(
    near_list, far_list, mid_list, root_list,
    points, charges, leaf_skel, mid_skel, root_skel, leaf_transfer, mid_transfer,
    out,
    win, cwin, mids, roots, rpart, yroots, src, chg, cof, fld, mtw, msrc, mcof, rsrc, rcof, rsk,
    send, recv,
):
    leaf, sub = lax.axis_index("leaf"), lax.axis_index("sub")
    leaves = charges.shape[0]
    my_mids = mid_transfer.shape[0]
    window = 3 * leaves
    group = SUBS * my_mids
    flat = leaf * SUBS + sub
    start = (flat - 1) * leaves
    total = XS * ZS * YS * SUBS
    rank_scale = 1.0 / leaf_transfer.shape[1]
    leaf_scale = 1.0 / math.sqrt(charges.shape[2])
    x, z, y = leaf // (ZS * YS), (leaf // YS) % ZS, leaf % YS
    right, left = (flat + 1) % total, (flat + total - 1) % total
    right_id, left_id = (right // SUBS, right % SUBS), (left // SUBS, left % SUBS)
    sub_ids = [(leaf, (sub + k) % SUBS) for k in range(1, SUBS)]
    y_ids = [(leaf - y + (y + k) % YS, sub) for k in range(1, YS)]
    z_ids = [((x * ZS + (z + k) % ZS) * YS + y, sub) for k in range(1, ZS)]
    x_id = (((1 - x) * ZS + z) * YS + y, sub)

    barrier = pltpu.get_barrier_semaphore()
    partners = [right_id, left_id] + sub_ids + y_ids + z_ids + [x_id]
    for partner in partners:
        pl.semaphore_signal(barrier, inc=1, device_id=partner, device_id_type=MESH)

    def copy(slot, source, target_ref, target):
        return pltpu.make_async_remote_copy(
            src_ref=source, dst_ref=target_ref, send_sem=send.at[slot], recv_sem=recv.at[slot],
            device_id=target, device_id_type=MESH,
        )

    def halo(slot, ref):
        own = ref.at[pl.ds(leaves, leaves)]
        return [
            copy(slot, own, ref.at[pl.ds(0, leaves)], right_id),
            copy(slot + 1, own, ref.at[pl.ds(2 * leaves, leaves)], left_id),
        ]

    half = low_half((8, 128))
    lane48 = low_half((48, 128))
    lane16 = low_half((16, 128))
    zero = jnp.zeros((16, 128), BF)

    own_rows = pl.ds(leaves, leaves)
    for r, value in enumerate(centred([points[c] for c in range(3)])):
        win[own_rows, r, :] = value
    for r, value in enumerate(centred([doubled(leaf_skel[c]) for c in range(3)])):
        win[own_rows, 4 + r, :] = value
    win[own_rows, pl.ds(8, 8), :] = charges[...]
    own_mid_rows = pl.ds(sub * my_mids, my_mids)
    for r, value in enumerate(centred([doubled(mid_skel[c]) for c in range(3)])):
        mids[own_mid_rows, 8 + r, :] = value
        mids[own_mid_rows, 12 + r, :] = value

    def one_leaf(i, carry):
        w = win[leaves + i]
        rows = source_rows(w[:8])
        two = stacked(w[8:])
        src[leaves + i] = rows
        chg[leaves + i] = two
        skel = jnp.concatenate([w[4:8], w[4:8]], axis=0)
        tgt = target_rows(skel, True).astype(BF)
        d2 = lax.dot_general(rows, tgt, TT, preferred_element_type=F32)
        coeff = split_dot(two, lax.rsqrt(d2), NN) * leaf_scale
        cwin[leaves + i] = coeff
        cof[leaves + i] = stacked(coeff)
        return carry

    lax.fori_loop(0, leaves // 2, one_leaf, 0, unroll=4)
    pl.semaphore_wait(barrier, len(partners))
    points_halo = halo(6, win)
    for c in points_halo:
        c.start()
    lax.fori_loop(leaves // 2, leaves, one_leaf, 0, unroll=4)
    coeff_halo = halo(8, cwin)
    for c in coeff_halo:
        c.start()

    def lifted(low_child, high_child, pair):
        both = jnp.where(half, low_child, high_child)
        return split_dot(stacked(both), doubled(pair.reshape(128, 64)), NN)

    mid_coeffs = []
    for m in range(my_mids):
        acc = jnp.zeros((8, 128), F32)
        for k in range(0, 8, 2):
            c = m * 8 + k
            acc += lifted(cwin[leaves + c], cwin[leaves + c + 1], leaf_transfer[c : c + 2])
        mid_coeffs.append(acc)
        mids[sub * my_mids + m, pl.ds(0, 8), :] = acc
    partial = jnp.zeros((8, 128), F32)
    for m in range(0, my_mids, 2):
        partial += lifted(mid_coeffs[m], mid_coeffs[m + 1], mid_transfer[m : m + 2])
    rpart[sub] = partial
    own_mids = mids.at[own_mid_rows]
    mid_copies = [copy(3 + k, own_mids, own_mids, sub_ids[k]) for k in range(3)]
    sums = [copy(k, rpart.at[sub], rpart.at[sub], sub_ids[k]) for k in range(3)]
    for c in mid_copies + sums:
        c.start()

    src[window] = src[leaves]
    chg[window] = zero
    cof[window] = zero
    for c in range(3):
        rsk[c] = doubled(root_skel[c].T)

    for c in points_halo:
        c.wait()

    def build(j, carry):
        for k in (j, 2 * leaves + j):
            w = win[k]
            src[k] = source_rows(w[:8])
            chg[k] = stacked(w[8:])
        return carry

    lax.fori_loop(0, leaves, build, 0, unroll=2)

    def place(j, first, empty):
        return jnp.where(j >= 0, jnp.clip(j - first, 0, empty - 1), empty)

    def near_leaves(t, carry):
        ids = [t * LP + p for p in range(LP)]
        tgts = [target_rows(win[leaves + i][:8], True).T.astype(BF) for i in ids]
        accs = [jnp.zeros((16, 128), F32)] * LP
        count = near_list.shape[1]
        for g in range(0, count, 2):
            for p, i in enumerate(ids):
                js = [place(near_list[i, k], start, window) for k in range(g, min(g + 2, count))]
                s = jnp.concatenate([src[j] for j in js], axis=1)
                q = jnp.concatenate([chg[j] for j in js], axis=1)
                d2 = lax.dot_general(s, tgts[p], TN, preferred_element_type=F32)
                high, low = split2(lax.rsqrt(d2))
                accs[p] += jnp.dot(q, high, preferred_element_type=F32) + jnp.dot(
                    q, low, preferred_element_type=F32
                )
        for p, i in enumerate(ids):
            out[i] = (accs[p][:8] + accs[p][8:]) * (1.0 / 128.0)
        return carry

    for c in sums:
        c.wait()
    yroots[y] = (rpart[0] + rpart[1]) + (rpart[2] + rpart[3])
    stage = [copy(10 + k, yroots.at[y], yroots.at[y], y_ids[k]) for k in range(YS - 1)]
    for c in stage:
        c.start()
    lax.fori_loop(0, 1, near_leaves, 0)
    for c in stage:
        c.wait()
    roots[x, z, 0] = jnp.where(half, yroots[0], yroots[1])
    roots[x, z, 1] = jnp.where(half, yroots[2], yroots[3])
    own = roots.at[x, z]
    stage = [copy(13 + k, own, own, z_ids[k]) for k in range(ZS - 1)]
    for c in stage:
        c.start()
    lax.fori_loop(1, 4, near_leaves, 0)
    for c in stage:
        c.wait()
    last = copy(28, roots.at[x], roots.at[x], x_id)
    last.start()
    lax.fori_loop(4, leaves // LP, near_leaves, 0)

    for c in coeff_halo + mid_copies:
        c.wait()

    def build_coeffs(j, carry):
        for k in (j, 2 * leaves + j):
            cof[k] = stacked(cwin[k])
        return carry

    lax.fori_loop(0, leaves, build_coeffs, 0, unroll=4)
    for j in range(group):
        w = mids[j]
        msrc[j] = source_rows(w[8:])
        mcof[j] = stacked(w[:8])
    msrc[group] = msrc[0]
    mcof[group] = zero

    def far_targets(p8):
        rows = target_rows(p8, False)
        low = low_half(rows.shape)
        pair = jnp.concatenate([jnp.where(low, rows, 0.0), jnp.where(low, 0.0, rows)], axis=0)
        return pair.T.astype(BF)

    def quad(js, table, coeffs, tgt):
        a, b, c, d = js
        s = jnp.concatenate(
            [jnp.where(lane48, table[a], table[c]), jnp.where(lane48, table[b], table[d])], axis=0
        )
        q = jnp.concatenate(
            [jnp.where(lane16, coeffs[a], coeffs[c]), jnp.where(lane16, coeffs[b], coeffs[d])],
            axis=0,
        )
        high, low = split2(lax.rsqrt(lax.dot_general(s, tgt, TN, preferred_element_type=F32)))
        return jnp.dot(q, high, preferred_element_type=F32) + jnp.dot(
            q, low, preferred_element_type=F32
        )

    def field(acc):
        s = jnp.where(half, acc[0:8] + acc[8:16], acc[16:24] + acc[24:32])
        return (s + pltpu.roll(s, 64, 1)) * rank_scale

    def far_leaves(t, carry):
        ids = [t * LP + p for p in range(LP)]
        tgts = [far_targets(win[leaves + i][:8]) for i in ids]
        accs = [jnp.zeros((32, 128), F32)] * LP
        for g in range(0, far_list.shape[0], 4):
            for p, i in enumerate(ids):
                js = [place(far_list[g + k, i], start, window) for k in range(4)]
                accs[p] += quad(js, src, cof, tgts[p])
        for p, i in enumerate(ids):
            fld[i] = field(accs[p])
        return carry

    lax.fori_loop(0, leaves // LP, far_leaves, 0)
    mid_fields = []
    for m in range(my_mids):
        js = [place(mid_list[m, k], leaf * group, group) for k in range(mid_list.shape[1])]
        js += [group] * (8 - len(js))
        tgt = far_targets(mids[sub * my_mids + m, pl.ds(8, 8), :])
        mid_fields.append(
            field(quad(js[:4], msrc, mcof, tgt) + quad(js[4:], msrc, mcof, tgt))
        )

    def root_p8(r):
        rows = centred([rsk[c, pl.ds(r, 1), :] for c in range(3)])
        return jnp.concatenate(rows + rows, axis=0)

    last.wait()
    slots = root_list.shape[1]
    for k in range(slots):
        r = root_list[0, k]
        present = (r >= 0).astype(F32)
        r = jnp.maximum(r, 0)
        tile = roots[r // (2 * ZS * 2), (r // YS) % ZS, (r // 2) % 2]
        mine = (lax.broadcasted_iota(jnp.int32, (8, 128), 1) // 64) == (r % 2)
        coeff = jnp.where(mine, tile, pltpu.roll(tile, 64, 1))
        rsrc[k] = source_rows(root_p8(r))
        rcof[k] = stacked(coeff * present)
    for k in range(slots, 8):
        rsrc[k] = rsrc[0]
        rcof[k] = zero
    tgt = far_targets(root_p8(leaf))
    acc = quad((0, 1, 2, 3), rsrc, rcof, tgt) + quad((4, 5, 6, 7), rsrc, rcof, tgt)
    root_two = stacked(field(acc))[:, :64]
    for m in range(my_mids):
        value = mid_fields[m][:, :64] + split_dot(root_two, mid_transfer[m], NT)
        mtw[m] = stacked(value)

    def finish(t, carry):
        for p in range(LP):
            i = t * LP + p
            lowered = split_dot(mtw[i // 8], leaf_transfer[i], NT)
            two = stacked((fld[i][:, :64] + lowered) * leaf_scale)
            w = win[leaves + i]
            own = jnp.concatenate([w[:4], w[:4]], axis=0)
            basis = target_rows(own, False).T.astype(BF)
            d2 = lax.dot_general(src[leaves + i][:, :64], basis, TN, preferred_element_type=F32)
            out[i] += split_dot(two, lax.rsqrt(d2), NN)
        return carry

    lax.fori_loop(0, leaves // LP, finish, 0)


def local(
    points, charges, leaf_skel, mid_skel, root_skel, leaf_transfer, mid_transfer,
    near_list, far_list, mid_list, root_list,
):
    leaves = points.shape[0]
    mids = mid_skel.shape[0]
    window = 3 * leaves + 1
    group = SUBS * mids + 1
    vmem = pl.BlockSpec(memory_space=pltpu.VMEM)
    smem = pl.BlockSpec(memory_space=pltpu.SMEM)
    return pl.pallas_call(
        body,
        name="h2_product",
        out_shape=jax.ShapeDtypeStruct((leaves, 8, 128), F32),
        in_specs=[smem] * 4 + [vmem] * 7,
        out_specs=vmem,
        scratch_shapes=[
            pltpu.VMEM((3 * leaves, 16, 128), F32),
            pltpu.VMEM((3 * leaves, 8, 128), F32),
            pltpu.VMEM((SUBS * mids, 16, 128), F32),
            pltpu.VMEM((XS, ZS, YS // 2, 8, 128), F32),
            pltpu.VMEM((SUBS, 8, 128), F32),
            pltpu.VMEM((YS, 8, 128), F32),
            pltpu.VMEM((window, 48, 128), BF),
            pltpu.VMEM((window, 16, 128), BF),
            pltpu.VMEM((window, 16, 128), BF),
            pltpu.VMEM((leaves, 8, 128), F32),
            pltpu.VMEM((mids, 16, 64), BF),
            pltpu.VMEM((group, 48, 128), BF),
            pltpu.VMEM((group, 16, 128), BF),
            pltpu.VMEM((8, 48, 128), BF),
            pltpu.VMEM((8, 16, 128), BF),
            pltpu.VMEM((3, XS * ZS * YS, 128), F32),
            pltpu.SemaphoreType.DMA((29,)),
            pltpu.SemaphoreType.DMA((29,)),
        ],
        compiler_params=pltpu.CompilerParams(collective_id=0, has_side_effects=True),
    )(
        near_list, far_list.T, mid_list, root_list,
        points.transpose(1, 0, 2), charges, leaf_skel.transpose(1, 0, 2),
        mid_skel.transpose(1, 0, 2), root_skel.transpose(1, 2, 0), leaf_transfer, mid_transfer,
    )


def solution(mesh):
    both = P(("leaf", "sub"), None, None)
    lists = P(("leaf", "sub"), None)
    in_specs = (both, both, both, both, P(), both, both, lists, lists, lists, P("leaf", None))
    return jax.shard_map(local, mesh=mesh, in_specs=in_specs, out_specs=both, check_vma=False)
```

```python
import functools
import math

import jax
import jax.numpy as jnp
from jax import lax
from jax.experimental import pallas as pl
from jax.experimental.pallas import tpu as pltpu
from jax.sharding import PartitionSpec as P

DELTA2 = 0.0025
MESH = pl.DeviceIdType.MESH
BF = jnp.bfloat16
F32 = jnp.float32
TN = (((0,), (1,)), ((), ()))
TT = (((0,), (0,)), ((), ()))
NT = (((1,), (1,)), ((), ()))
YS, ZS, XS, SUBS = 4, 16, 2, 4


def rows_of(x):
    return lax.broadcasted_iota(jnp.int32, x.shape, 0)


def low_half(shape):
    return lax.broadcasted_iota(jnp.int32, shape, len(shape) - 1) < 64


def split2(x):
    high = x.astype(BF)
    return high, (x - high.astype(F32)).astype(BF)


def stacked(x):
    high = x.astype(BF).astype(F32)
    return jnp.concatenate([high, x - high], axis=0).astype(BF)


def split3(x):
    first = x.astype(BF).astype(F32)
    rest = x - first
    second = rest.astype(BF).astype(F32)
    return first, second, (rest - second).astype(BF).astype(F32)


def centred(rows):
    c = [r - 0.5 for r in rows]
    return c + [c[0] * c[0] + c[1] * c[1] + c[2] * c[2] + 0.5 * DELTA2]


def doubled(s):
    return jnp.concatenate([s, s], axis=1)


def source_rows(p8):
    p1, p2, p3 = split3(p8)
    norm = (rows_of(p8) & 3) == 3
    ones = jnp.where(norm, 1.0, p1)
    return jnp.concatenate([p1, p2, p3, ones, jnp.where(norm, 1.0, p2), ones], axis=0).astype(BF)


def target_rows(p8, first_half):
    p1, p2, p3 = split3(p8)
    row = rows_of(p8)
    norm = (row & 3) == 3
    active = ((row < 4) if first_half else (row >= 4)).astype(F32)
    lead = jnp.where(norm, 1.0, -2.0 * p1) * active
    return jnp.concatenate(
        [
            lead,
            lead,
            lead,
            jnp.where(norm, p1, -2.0 * p2) * active,
            jnp.where(norm, p2, -2.0 * p2) * active,
            jnp.where(norm, p3, -2.0 * p3) * active,
        ],
        axis=0,
    )


def split_dot(two, matrix, dims):
    high, low = split2(matrix)
    out = lax.dot_general(two, high, dims, preferred_element_type=F32) + lax.dot_general(
        two, low, dims, preferred_element_type=F32
    )
    half = out.shape[0] // 2
    return out[:half] + out[half:]


NN = (((1,), (0,)), ((), ()))
LP = 4


def body(
    near_list, far_list, mid_list, root_list,
    points, charges, leaf_skel, mid_skel, root_skel, leaf_transfer, mid_transfer,
    out,
    win, cwin, mids, roots, rpart, yroots, src, chg, cof, fld, mtw, msrc, mcof, rsrc, rcof, rsk,
    send, recv,
):
    leaf, sub = lax.axis_index("leaf"), lax.axis_index("sub")
    leaves = charges.shape[0]
    my_mids = mid_transfer.shape[0]
    window = 3 * leaves
    group = SUBS * my_mids
    flat = leaf * SUBS + sub
    start = (flat - 1) * leaves
    total = XS * ZS * YS * SUBS
    rank_scale = 1.0 / leaf_transfer.shape[1]
    leaf_scale = 1.0 / math.sqrt(charges.shape[2])
    x, z, y = leaf // (ZS * YS), (leaf // YS) % ZS, leaf % YS
    right, left = (flat + 1) % total, (flat + total - 1) % total
    right_id, left_id = (right // SUBS, right % SUBS), (left // SUBS, left % SUBS)
    sub_ids = [(leaf, (sub + k) % SUBS) for k in range(1, SUBS)]
    y_ids = [(leaf - y + (y + k) % YS, sub) for k in range(1, YS)]
    z_ids = [((x * ZS + (z + k) % ZS) * YS + y, sub) for k in range(1, ZS)]
    x_id = (((1 - x) * ZS + z) * YS + y, sub)

    barrier = pltpu.get_barrier_semaphore()
    partners = [right_id, left_id] + sub_ids + y_ids + z_ids + [x_id]
    for partner in partners:
        pl.semaphore_signal(barrier, inc=1, device_id=partner, device_id_type=MESH)

    def copy(slot, source, target_ref, target):
        return pltpu.make_async_remote_copy(
            src_ref=source, dst_ref=target_ref, send_sem=send.at[slot], recv_sem=recv.at[slot],
            device_id=target, device_id_type=MESH,
        )

    def halo(slot, ref):
        own = ref.at[pl.ds(leaves, leaves)]
        return [
            copy(slot, own, ref.at[pl.ds(0, leaves)], right_id),
            copy(slot + 1, own, ref.at[pl.ds(2 * leaves, leaves)], left_id),
        ]

    half = low_half((8, 128))
    lane48 = low_half((48, 128))
    lane16 = low_half((16, 128))
    zero = jnp.zeros((16, 128), BF)

    own_rows = pl.ds(leaves, leaves)
    for r, value in enumerate(centred([points[c] for c in range(3)])):
        win[own_rows, r, :] = value
    for r, value in enumerate(centred([doubled(leaf_skel[c]) for c in range(3)])):
        win[own_rows, 4 + r, :] = value
    win[own_rows, pl.ds(8, 8), :] = charges[...]
    own_mid_rows = pl.ds(sub * my_mids, my_mids)
    for r, value in enumerate(centred([doubled(mid_skel[c]) for c in range(3)])):
        mids[own_mid_rows, 8 + r, :] = value
        mids[own_mid_rows, 12 + r, :] = value

    def one_leaf(i, carry):
        w = win[leaves + i]
        rows = source_rows(w[:8])
        two = stacked(w[8:])
        src[leaves + i] = rows
        chg[leaves + i] = two
        skel = jnp.concatenate([w[4:8], w[4:8]], axis=0)
        tgt = target_rows(skel, True).astype(BF)
        d2 = lax.dot_general(rows, tgt, TT, preferred_element_type=F32)
        coeff = split_dot(two, lax.rsqrt(d2), NN) * leaf_scale
        cwin[leaves + i] = coeff
        cof[leaves + i] = stacked(coeff)
        return carry

    lax.fori_loop(0, leaves // 2, one_leaf, 0, unroll=4)
    pl.semaphore_wait(barrier, len(partners))
    points_halo = halo(6, win)
    for c in points_halo:
        c.start()
    lax.fori_loop(leaves // 2, leaves, one_leaf, 0, unroll=4)
    def lifted(low_child, high_child, pair):
        both = jnp.where(half, low_child, high_child)
        return split_dot(stacked(both), doubled(pair.reshape(128, 64)), NN)

    mid_coeffs = []
    for m in range(my_mids):
        acc = jnp.zeros((8, 128), F32)
        for k in range(0, 8, 2):
            c = m * 8 + k
            acc += lifted(cwin[leaves + c], cwin[leaves + c + 1], leaf_transfer[c : c + 2])
        mid_coeffs.append(acc)
        mids[sub * my_mids + m, pl.ds(0, 8), :] = acc
    partial = jnp.zeros((8, 128), F32)
    for m in range(0, my_mids, 2):
        partial += lifted(mid_coeffs[m], mid_coeffs[m + 1], mid_transfer[m : m + 2])
    rpart[sub] = partial
    own_mids = mids.at[own_mid_rows]
    mid_copies = [copy(3 + k, own_mids, own_mids, sub_ids[k]) for k in range(3)]
    sums = [copy(k, rpart.at[sub], rpart.at[sub], sub_ids[k]) for k in range(3)]
    for c in sums + mid_copies:
        c.start()

    src[window] = src[leaves]
    chg[window] = zero
    cof[window] = zero
    for c in range(3):
        rsk[c] = doubled(root_skel[c].T)

    for c in points_halo:
        c.wait()

    def build(j, carry):
        for k in (j, 2 * leaves + j):
            w = win[k]
            src[k] = source_rows(w[:8])
            chg[k] = stacked(w[8:])
        return carry

    lax.fori_loop(0, leaves, build, 0, unroll=2)

    def place(j, first, empty):
        return jnp.where(j >= 0, jnp.clip(j - first, 0, empty - 1), empty)

    def near_leaves(t, carry):
        ids = [t * LP + p for p in range(LP)]
        tgts = [target_rows(win[leaves + i][:8], True).T.astype(BF) for i in ids]
        accs = [jnp.zeros((16, 128), F32)] * LP
        count = near_list.shape[1]
        for g in range(0, count, 2):
            for p, i in enumerate(ids):
                js = [place(near_list[i, k], start, window) for k in range(g, min(g + 2, count))]
                s = jnp.concatenate([src[j] for j in js], axis=1)
                q = jnp.concatenate([chg[j] for j in js], axis=1)
                d2 = lax.dot_general(s, tgts[p], TN, preferred_element_type=F32)
                high, low = split2(lax.rsqrt(d2))
                accs[p] += jnp.dot(q, high, preferred_element_type=F32) + jnp.dot(
                    q, low, preferred_element_type=F32
                )
        for p, i in enumerate(ids):
            out[i] = (accs[p][:8] + accs[p][8:]) * (1.0 / 128.0)
        return carry

    lax.fori_loop(0, 1, near_leaves, 0)
    for c in sums:
        c.wait()
    yroots[y] = (rpart[0] + rpart[1]) + (rpart[2] + rpart[3])
    stage = [copy(10 + k, yroots.at[y], yroots.at[y], y_ids[k]) for k in range(YS - 1)]
    for c in stage:
        c.start()
    lax.fori_loop(1, 2, near_leaves, 0)
    for c in stage:
        c.wait()
    roots[x, z, 0] = jnp.where(half, yroots[0], yroots[1])
    roots[x, z, 1] = jnp.where(half, yroots[2], yroots[3])
    own = roots.at[x, z]
    stage = [copy(13 + k, own, own, z_ids[k]) for k in range(ZS - 1)]
    for c in stage:
        c.start()
    coeff_halo = halo(8, cwin)
    for c in coeff_halo:
        c.start()
    lax.fori_loop(2, 6, near_leaves, 0)
    for c in stage:
        c.wait()
    last = copy(28, roots.at[x], roots.at[x], x_id)
    last.start()
    lax.fori_loop(6, leaves // LP, near_leaves, 0)

    for c in coeff_halo + mid_copies:
        c.wait()

    def build_coeffs(j, carry):
        for k in (j, 2 * leaves + j):
            cof[k] = stacked(cwin[k])
        return carry

    lax.fori_loop(0, leaves, build_coeffs, 0, unroll=4)
    for j in range(group):
        w = mids[j]
        msrc[j] = source_rows(w[8:])
        mcof[j] = stacked(w[:8])
    msrc[group] = msrc[0]
    mcof[group] = zero

    def far_targets(p8):
        rows = target_rows(p8, False)
        low = low_half(rows.shape)
        pair = jnp.concatenate([jnp.where(low, rows, 0.0), jnp.where(low, 0.0, rows)], axis=0)
        return pair.T.astype(BF)

    def quad(js, table, coeffs, tgt):
        a, b, c, d = js
        s = jnp.concatenate(
            [jnp.where(lane48, table[a], table[c]), jnp.where(lane48, table[b], table[d])], axis=0
        )
        q = jnp.concatenate(
            [jnp.where(lane16, coeffs[a], coeffs[c]), jnp.where(lane16, coeffs[b], coeffs[d])],
            axis=0,
        )
        high, low = split2(lax.rsqrt(lax.dot_general(s, tgt, TN, preferred_element_type=F32)))
        return jnp.dot(q, high, preferred_element_type=F32) + jnp.dot(
            q, low, preferred_element_type=F32
        )

    def field(acc):
        s = jnp.where(half, acc[0:8] + acc[8:16], acc[16:24] + acc[24:32])
        return (s + pltpu.roll(s, 64, 1)) * rank_scale

    def far_leaves(t, carry):
        ids = [t * LP + p for p in range(LP)]
        tgts = [far_targets(win[leaves + i][:8]) for i in ids]
        accs = [jnp.zeros((32, 128), F32)] * LP
        for g in range(0, far_list.shape[0], 4):
            for p, i in enumerate(ids):
                js = [place(far_list[g + k, i], start, window) for k in range(4)]
                accs[p] += quad(js, src, cof, tgts[p])
        for p, i in enumerate(ids):
            fld[i] = field(accs[p])
        return carry

    lax.fori_loop(0, leaves // LP, far_leaves, 0)
    mid_fields = []
    for m in range(my_mids):
        js = [place(mid_list[m, k], leaf * group, group) for k in range(mid_list.shape[1])]
        js += [group] * (8 - len(js))
        tgt = far_targets(mids[sub * my_mids + m, pl.ds(8, 8), :])
        mid_fields.append(
            field(quad(js[:4], msrc, mcof, tgt) + quad(js[4:], msrc, mcof, tgt))
        )

    def root_p8(r):
        rows = centred([rsk[c, pl.ds(r, 1), :] for c in range(3)])
        return jnp.concatenate(rows + rows, axis=0)

    last.wait()
    slots = root_list.shape[1]
    for k in range(slots):
        r = root_list[0, k]
        present = (r >= 0).astype(F32)
        r = jnp.maximum(r, 0)
        tile = roots[r // (2 * ZS * 2), (r // YS) % ZS, (r // 2) % 2]
        mine = (lax.broadcasted_iota(jnp.int32, (8, 128), 1) // 64) == (r % 2)
        coeff = jnp.where(mine, tile, pltpu.roll(tile, 64, 1))
        rsrc[k] = source_rows(root_p8(r))
        rcof[k] = stacked(coeff * present)
    for k in range(slots, 8):
        rsrc[k] = rsrc[0]
        rcof[k] = zero
    tgt = far_targets(root_p8(leaf))
    acc = quad((0, 1, 2, 3), rsrc, rcof, tgt) + quad((4, 5, 6, 7), rsrc, rcof, tgt)
    root_two = stacked(field(acc))[:, :64]
    for m in range(my_mids):
        value = mid_fields[m][:, :64] + split_dot(root_two, mid_transfer[m], NT)
        mtw[m] = stacked(value)

    def finish(t, carry):
        for p in range(LP):
            i = t * LP + p
            lowered = split_dot(mtw[i // 8], leaf_transfer[i], NT)
            two = stacked((fld[i][:, :64] + lowered) * leaf_scale)
            w = win[leaves + i]
            own = jnp.concatenate([w[:4], w[:4]], axis=0)
            basis = target_rows(own, False).T.astype(BF)
            d2 = lax.dot_general(src[leaves + i][:, :64], basis, TN, preferred_element_type=F32)
            out[i] += split_dot(two, lax.rsqrt(d2), NN)
        return carry

    lax.fori_loop(0, leaves // LP, finish, 0)


def local(
    points, charges, leaf_skel, mid_skel, root_skel, leaf_transfer, mid_transfer,
    near_list, far_list, mid_list, root_list,
):
    leaves = points.shape[0]
    mids = mid_skel.shape[0]
    window = 3 * leaves + 1
    group = SUBS * mids + 1
    vmem = pl.BlockSpec(memory_space=pltpu.VMEM)
    smem = pl.BlockSpec(memory_space=pltpu.SMEM)
    return pl.pallas_call(
        body,
        name="h2_product",
        out_shape=jax.ShapeDtypeStruct((leaves, 8, 128), F32),
        in_specs=[smem] * 4 + [vmem] * 7,
        out_specs=vmem,
        scratch_shapes=[
            pltpu.VMEM((3 * leaves, 16, 128), F32),
            pltpu.VMEM((3 * leaves, 8, 128), F32),
            pltpu.VMEM((SUBS * mids, 16, 128), F32),
            pltpu.VMEM((XS, ZS, YS // 2, 8, 128), F32),
            pltpu.VMEM((SUBS, 8, 128), F32),
            pltpu.VMEM((YS, 8, 128), F32),
            pltpu.VMEM((window, 48, 128), BF),
            pltpu.VMEM((window, 16, 128), BF),
            pltpu.VMEM((window, 16, 128), BF),
            pltpu.VMEM((leaves, 8, 128), F32),
            pltpu.VMEM((mids, 16, 64), BF),
            pltpu.VMEM((group, 48, 128), BF),
            pltpu.VMEM((group, 16, 128), BF),
            pltpu.VMEM((8, 48, 128), BF),
            pltpu.VMEM((8, 16, 128), BF),
            pltpu.VMEM((3, XS * ZS * YS, 128), F32),
            pltpu.SemaphoreType.DMA((29,)),
            pltpu.SemaphoreType.DMA((29,)),
        ],
        compiler_params=pltpu.CompilerParams(collective_id=0, has_side_effects=True),
    )(
        near_list, far_list.T, mid_list, root_list,
        points.transpose(1, 0, 2), charges, leaf_skel.transpose(1, 0, 2),
        mid_skel.transpose(1, 0, 2), root_skel.transpose(1, 2, 0), leaf_transfer, mid_transfer,
    )


def solution(mesh):
    both = P(("leaf", "sub"), None, None)
    lists = P(("leaf", "sub"), None)
    in_specs = (both, both, both, both, P(), both, both, lists, lists, lists, P("leaf", None))
    return jax.shard_map(local, mesh=mesh, in_specs=in_specs, out_specs=both, check_vma=False)
```

```python
import functools
import math

import jax
import jax.numpy as jnp
from jax import lax
from jax.experimental import pallas as pl
from jax.experimental.pallas import tpu as pltpu
from jax.sharding import PartitionSpec as P

DELTA2 = 0.0025
MESH = pl.DeviceIdType.MESH
BF = jnp.bfloat16
F32 = jnp.float32
TN = (((0,), (1,)), ((), ()))
TT = (((0,), (0,)), ((), ()))
NT = (((1,), (1,)), ((), ()))
YS, ZS, XS, SUBS = 4, 16, 2, 4


def rows_of(x):
    return lax.broadcasted_iota(jnp.int32, x.shape, 0)


def low_half(shape):
    return lax.broadcasted_iota(jnp.int32, shape, len(shape) - 1) < 64


def split2(x):
    high = x.astype(BF)
    return high, (x - high.astype(F32)).astype(BF)


def stacked(x):
    high = x.astype(BF).astype(F32)
    return jnp.concatenate([high, x - high], axis=0).astype(BF)


def split3(x):
    first = x.astype(BF).astype(F32)
    rest = x - first
    second = rest.astype(BF).astype(F32)
    return first, second, (rest - second).astype(BF).astype(F32)


def centred(rows):
    c = [r - 0.5 for r in rows]
    return c + [c[0] * c[0] + c[1] * c[1] + c[2] * c[2] + 0.5 * DELTA2]


def doubled(s):
    return jnp.concatenate([s, s], axis=1)


def source_rows(p8):
    p1, p2, p3 = split3(p8)
    norm = (rows_of(p8) & 3) == 3
    ones = jnp.where(norm, 1.0, p1)
    return jnp.concatenate([p1, p2, p3, ones, jnp.where(norm, 1.0, p2), ones], axis=0).astype(BF)


def target_rows(p8, first_half):
    p1, p2, p3 = split3(p8)
    row = rows_of(p8)
    norm = (row & 3) == 3
    active = ((row < 4) if first_half else (row >= 4)).astype(F32)
    lead = jnp.where(norm, 1.0, -2.0 * p1) * active
    return jnp.concatenate(
        [
            lead,
            lead,
            lead,
            jnp.where(norm, p1, -2.0 * p2) * active,
            jnp.where(norm, p2, -2.0 * p2) * active,
            jnp.where(norm, p3, -2.0 * p3) * active,
        ],
        axis=0,
    )


def split_dot(two, matrix, dims):
    high, low = split2(matrix)
    out = lax.dot_general(two, high, dims, preferred_element_type=F32) + lax.dot_general(
        two, low, dims, preferred_element_type=F32
    )
    half = out.shape[0] // 2
    return out[:half] + out[half:]


NN = (((1,), (0,)), ((), ()))
LP = 4


def body(
    near_list, far_list, mid_list, root_list,
    points, charges, leaf_skel, mid_skel, root_skel, leaf_transfer, mid_transfer,
    out,
    win, cwin, mids, roots, rpart, yroots, src, chg, cof, fld, mtw, msrc, mcof, rsrc, rcof, rsk,
    send, recv,
):
    leaf, sub = lax.axis_index("leaf"), lax.axis_index("sub")
    leaves = charges.shape[0]
    my_mids = mid_transfer.shape[0]
    window = 3 * leaves
    group = SUBS * my_mids
    flat = leaf * SUBS + sub
    start = (flat - 1) * leaves
    total = XS * ZS * YS * SUBS
    rank_scale = 1.0 / leaf_transfer.shape[1]
    leaf_scale = 1.0 / math.sqrt(charges.shape[2])
    x, z, y = leaf // (ZS * YS), (leaf // YS) % ZS, leaf % YS
    right, left = (flat + 1) % total, (flat + total - 1) % total
    right_id, left_id = (right // SUBS, right % SUBS), (left // SUBS, left % SUBS)
    sub_ids = [(leaf, (sub + k) % SUBS) for k in range(1, SUBS)]
    y_ids = [(leaf - y + (y + k) % YS, sub) for k in range(1, YS)]
    z_ids = [((x * ZS + (z + k) % ZS) * YS + y, sub) for k in range(1, ZS)]
    x_id = (((1 - x) * ZS + z) * YS + y, sub)

    barrier = pltpu.get_barrier_semaphore()
    partners = [right_id, left_id] + sub_ids + y_ids + z_ids + [x_id]
    for partner in partners:
        pl.semaphore_signal(barrier, inc=1, device_id=partner, device_id_type=MESH)

    def copy(slot, source, target_ref, target):
        return pltpu.make_async_remote_copy(
            src_ref=source, dst_ref=target_ref, send_sem=send.at[slot], recv_sem=recv.at[slot],
            device_id=target, device_id_type=MESH,
        )

    def halo(slot, ref):
        own = ref.at[pl.ds(leaves, leaves)]
        return [
            copy(slot, own, ref.at[pl.ds(0, leaves)], right_id),
            copy(slot + 1, own, ref.at[pl.ds(2 * leaves, leaves)], left_id),
        ]

    half = low_half((8, 128))
    lane48 = low_half((48, 128))
    lane16 = low_half((16, 128))
    zero = jnp.zeros((16, 128), BF)

    own_rows = pl.ds(leaves, leaves)
    for r, value in enumerate(centred([points[c] for c in range(3)])):
        win[own_rows, r, :] = value
    for r, value in enumerate(centred([doubled(leaf_skel[c]) for c in range(3)])):
        win[own_rows, 4 + r, :] = value
    win[own_rows, pl.ds(8, 8), :] = charges[...]
    own_mid_rows = pl.ds(sub * my_mids, my_mids)
    for r, value in enumerate(centred([doubled(mid_skel[c]) for c in range(3)])):
        mids[own_mid_rows, 8 + r, :] = value
        mids[own_mid_rows, 12 + r, :] = value

    def some_leaves(t, carry):
        ids = [leaves + t * LP + p for p in range(LP)]
        ws = [win[i] for i in ids]
        rows = [source_rows(w[:8]) for w in ws]
        twos = [stacked(w[8:]) for w in ws]
        tgts = [
            target_rows(jnp.concatenate([w[4:8], w[4:8]], axis=0), True).astype(BF) for w in ws
        ]
        d2 = [
            lax.dot_general(r, g, TT, preferred_element_type=F32) for r, g in zip(rows, tgts)
        ]
        basis = [lax.rsqrt(d) for d in d2]
        coeffs = [split_dot(two, g, NN) * leaf_scale for two, g in zip(twos, basis)]
        for i, r, two, coeff in zip(ids, rows, twos, coeffs):
            src[i] = r
            chg[i] = two
            cwin[i] = coeff
            cof[i] = stacked(coeff)
        return carry

    lax.fori_loop(0, leaves // (2 * LP), some_leaves, 0)
    pl.semaphore_wait(barrier, len(partners))
    points_halo = halo(6, win)
    for c in points_halo:
        c.start()
    lax.fori_loop(leaves // (2 * LP), leaves // LP, some_leaves, 0)
    def lifted(low_child, high_child, pair):
        both = jnp.where(half, low_child, high_child)
        return split_dot(stacked(both), doubled(pair.reshape(128, 64)), NN)

    mid_coeffs = []
    for m in range(my_mids):
        acc = jnp.zeros((8, 128), F32)
        for k in range(0, 8, 2):
            c = m * 8 + k
            acc += lifted(cwin[leaves + c], cwin[leaves + c + 1], leaf_transfer[c : c + 2])
        mid_coeffs.append(acc)
        mids[sub * my_mids + m, pl.ds(0, 8), :] = acc
    partial = jnp.zeros((8, 128), F32)
    for m in range(0, my_mids, 2):
        partial += lifted(mid_coeffs[m], mid_coeffs[m + 1], mid_transfer[m : m + 2])
    rpart[sub] = partial
    own_mids = mids.at[own_mid_rows]
    mid_copies = [copy(3 + k, own_mids, own_mids, sub_ids[k]) for k in range(3)]
    sums = [copy(k, rpart.at[sub], rpart.at[sub], sub_ids[k]) for k in range(3)]
    for c in sums + mid_copies:
        c.start()

    src[window] = src[leaves]
    chg[window] = zero
    cof[window] = zero
    for c in range(3):
        rsk[c] = doubled(root_skel[c].T)

    for c in points_halo:
        c.wait()

    def build(j, carry):
        for k in (j, 2 * leaves + j):
            w = win[k]
            src[k] = source_rows(w[:8])
            chg[k] = stacked(w[8:])
        return carry

    lax.fori_loop(0, leaves, build, 0, unroll=2)

    def place(j, first, empty):
        return jnp.where(j >= 0, jnp.clip(j - first, 0, empty - 1), empty)

    def near_leaves(t, carry):
        ids = [t * LP + p for p in range(LP)]
        tgts = [target_rows(win[leaves + i][:8], True).T.astype(BF) for i in ids]
        accs = [jnp.zeros((16, 128), F32)] * LP
        count = near_list.shape[1]
        for g in range(0, count, 2):
            for p, i in enumerate(ids):
                js = [place(near_list[i, k], start, window) for k in range(g, min(g + 2, count))]
                s = jnp.concatenate([src[j] for j in js], axis=1)
                q = jnp.concatenate([chg[j] for j in js], axis=1)
                d2 = lax.dot_general(s, tgts[p], TN, preferred_element_type=F32)
                high, low = split2(lax.rsqrt(d2))
                accs[p] += jnp.dot(q, high, preferred_element_type=F32) + jnp.dot(
                    q, low, preferred_element_type=F32
                )
        for p, i in enumerate(ids):
            out[i] = (accs[p][:8] + accs[p][8:]) * (1.0 / 128.0)
        return carry

    lax.fori_loop(0, 1, near_leaves, 0)
    for c in sums:
        c.wait()
    yroots[y] = (rpart[0] + rpart[1]) + (rpart[2] + rpart[3])
    stage = [copy(10 + k, yroots.at[y], yroots.at[y], y_ids[k]) for k in range(YS - 1)]
    for c in stage:
        c.start()
    lax.fori_loop(1, 2, near_leaves, 0)
    for c in stage:
        c.wait()
    roots[x, z, 0] = jnp.where(half, yroots[0], yroots[1])
    roots[x, z, 1] = jnp.where(half, yroots[2], yroots[3])
    own = roots.at[x, z]
    stage = [copy(13 + k, own, own, z_ids[k]) for k in range(ZS - 1)]
    for c in stage:
        c.start()
    coeff_halo = halo(8, cwin)
    for c in coeff_halo:
        c.start()
    lax.fori_loop(2, 6, near_leaves, 0)
    for c in stage:
        c.wait()
    last = copy(28, roots.at[x], roots.at[x], x_id)
    last.start()
    lax.fori_loop(6, leaves // LP, near_leaves, 0)

    for c in coeff_halo + mid_copies:
        c.wait()

    def build_coeffs(j, carry):
        for k in (j, 2 * leaves + j):
            cof[k] = stacked(cwin[k])
        return carry

    lax.fori_loop(0, leaves, build_coeffs, 0, unroll=4)
    for j in range(group):
        w = mids[j]
        msrc[j] = source_rows(w[8:])
        mcof[j] = stacked(w[:8])
    msrc[group] = msrc[0]
    mcof[group] = zero

    def far_targets(p8):
        rows = target_rows(p8, False)
        low = low_half(rows.shape)
        pair = jnp.concatenate([jnp.where(low, rows, 0.0), jnp.where(low, 0.0, rows)], axis=0)
        return pair.T.astype(BF)

    def quad(js, table, coeffs, tgt):
        a, b, c, d = js
        s = jnp.concatenate(
            [jnp.where(lane48, table[a], table[c]), jnp.where(lane48, table[b], table[d])], axis=0
        )
        q = jnp.concatenate(
            [jnp.where(lane16, coeffs[a], coeffs[c]), jnp.where(lane16, coeffs[b], coeffs[d])],
            axis=0,
        )
        high, low = split2(lax.rsqrt(lax.dot_general(s, tgt, TN, preferred_element_type=F32)))
        return jnp.dot(q, high, preferred_element_type=F32) + jnp.dot(
            q, low, preferred_element_type=F32
        )

    def field(acc):
        s = jnp.where(half, acc[0:8] + acc[8:16], acc[16:24] + acc[24:32])
        return (s + pltpu.roll(s, 64, 1)) * rank_scale

    def far_leaves(t, carry):
        ids = [t * LP + p for p in range(LP)]
        tgts = [far_targets(win[leaves + i][:8]) for i in ids]
        accs = [jnp.zeros((32, 128), F32)] * LP
        for g in range(0, far_list.shape[0], 4):
            for p, i in enumerate(ids):
                js = [place(far_list[g + k, i], start, window) for k in range(4)]
                accs[p] += quad(js, src, cof, tgts[p])
        for p, i in enumerate(ids):
            fld[i] = field(accs[p])
        return carry

    lax.fori_loop(0, leaves // LP, far_leaves, 0)
    mid_fields = []
    for m in range(my_mids):
        js = [place(mid_list[m, k], leaf * group, group) for k in range(mid_list.shape[1])]
        js += [group] * (8 - len(js))
        tgt = far_targets(mids[sub * my_mids + m, pl.ds(8, 8), :])
        mid_fields.append(
            field(quad(js[:4], msrc, mcof, tgt) + quad(js[4:], msrc, mcof, tgt))
        )

    def root_p8(r):
        rows = centred([rsk[c, pl.ds(r, 1), :] for c in range(3)])
        return jnp.concatenate(rows + rows, axis=0)

    last.wait()
    slots = root_list.shape[1]
    for k in range(slots):
        r = root_list[0, k]
        present = (r >= 0).astype(F32)
        r = jnp.maximum(r, 0)
        tile = roots[r // (2 * ZS * 2), (r // YS) % ZS, (r // 2) % 2]
        mine = (lax.broadcasted_iota(jnp.int32, (8, 128), 1) // 64) == (r % 2)
        coeff = jnp.where(mine, tile, pltpu.roll(tile, 64, 1))
        rsrc[k] = source_rows(root_p8(r))
        rcof[k] = stacked(coeff * present)
    for k in range(slots, 8):
        rsrc[k] = rsrc[0]
        rcof[k] = zero
    tgt = far_targets(root_p8(leaf))
    acc = quad((0, 1, 2, 3), rsrc, rcof, tgt) + quad((4, 5, 6, 7), rsrc, rcof, tgt)
    root_two = stacked(field(acc))[:, :64]
    for m in range(my_mids):
        value = mid_fields[m][:, :64] + split_dot(root_two, mid_transfer[m], NT)
        mtw[m] = stacked(value)

    def finish(t, carry):
        ids = [t * LP + p for p in range(LP)]
        rows = [win[leaves + i][:4] for i in ids]
        tgts = [
            target_rows(jnp.concatenate([w, w], axis=0), False).T.astype(BF) for w in rows
        ]
        lowered = [split_dot(mtw[i // 8], leaf_transfer[i], NT) for i in ids]
        d2 = [
            lax.dot_general(src[leaves + i][:, :64], g, TN, preferred_element_type=F32)
            for i, g in zip(ids, tgts)
        ]
        basis = [lax.rsqrt(d) for d in d2]
        twos = [stacked((fld[i][:, :64] + w) * leaf_scale) for i, w in zip(ids, lowered)]
        terms = [split_dot(two, g, NN) for two, g in zip(twos, basis)]
        for i, term in zip(ids, terms):
            out[i] += term
        return carry

    lax.fori_loop(0, leaves // LP, finish, 0)


def local(
    points, charges, leaf_skel, mid_skel, root_skel, leaf_transfer, mid_transfer,
    near_list, far_list, mid_list, root_list,
):
    leaves = points.shape[0]
    mids = mid_skel.shape[0]
    window = 3 * leaves + 1
    group = SUBS * mids + 1
    vmem = pl.BlockSpec(memory_space=pltpu.VMEM)
    smem = pl.BlockSpec(memory_space=pltpu.SMEM)
    return pl.pallas_call(
        body,
        name="h2_product",
        out_shape=jax.ShapeDtypeStruct((leaves, 8, 128), F32),
        in_specs=[smem] * 4 + [vmem] * 7,
        out_specs=vmem,
        scratch_shapes=[
            pltpu.VMEM((3 * leaves, 16, 128), F32),
            pltpu.VMEM((3 * leaves, 8, 128), F32),
            pltpu.VMEM((SUBS * mids, 16, 128), F32),
            pltpu.VMEM((XS, ZS, YS // 2, 8, 128), F32),
            pltpu.VMEM((SUBS, 8, 128), F32),
            pltpu.VMEM((YS, 8, 128), F32),
            pltpu.VMEM((window, 48, 128), BF),
            pltpu.VMEM((window, 16, 128), BF),
            pltpu.VMEM((window, 16, 128), BF),
            pltpu.VMEM((leaves, 8, 128), F32),
            pltpu.VMEM((mids, 16, 64), BF),
            pltpu.VMEM((group, 48, 128), BF),
            pltpu.VMEM((group, 16, 128), BF),
            pltpu.VMEM((8, 48, 128), BF),
            pltpu.VMEM((8, 16, 128), BF),
            pltpu.VMEM((3, XS * ZS * YS, 128), F32),
            pltpu.SemaphoreType.DMA((29,)),
            pltpu.SemaphoreType.DMA((29,)),
        ],
        compiler_params=pltpu.CompilerParams(collective_id=0, has_side_effects=True),
    )(
        near_list, far_list.T, mid_list, root_list,
        points.transpose(1, 0, 2), charges, leaf_skel.transpose(1, 0, 2),
        mid_skel.transpose(1, 0, 2), root_skel.transpose(1, 2, 0), leaf_transfer, mid_transfer,
    )


def solution(mesh):
    both = P(("leaf", "sub"), None, None)
    lists = P(("leaf", "sub"), None)
    in_specs = (both, both, both, both, P(), both, both, lists, lists, lists, P("leaf", None))
    return jax.shard_map(local, mesh=mesh, in_specs=in_specs, out_specs=both, check_vma=False)
```
